32 devices in a mesh: section: 2 (over core), hid: 8 (over z, x), mod: 2 (over y).
Axes of the slice: x: 2, y: 2, z: 4, core: 2. Of those that a mesh axis runs over, the one named last changes fastest.
Arguments:
- tokens: float32 [2048, 5120], P(('section', 'hid'), 'mod'), may hold values from -200 to 200
- gain_first: float32 [5120], P('mod'), may hold values from 0.1 to 1.9
- gate_first: bfloat16 [5120, 13824], P('mod', 'hid'), may hold values from -0.078125 to 0.078125
- up_first: bfloat16 [5120, 13824], P('mod', 'hid'), may hold values from -0.078125 to 0.078125
- down_first: bfloat16 [13824, 5120], P('hid', 'mod'), may hold values from -0.0546875 to 0.0546875
- gain_second: float32 [5120], P('mod'), may hold values from 0.1 to 1.9
- gate_second: bfloat16 [5120, 13824], P('mod', ('section', 'hid')), may hold values from -0.078125 to 0.078125
- up_second: bfloat16 [5120, 13824], P('mod', ('section', 'hid')), may hold values from -0.078125 to 0.078125
- down_second: bfloat16 [13824, 5120], P(('section', 'hid'), 'mod'), may hold values from -0.0546875 to 0.0546875
Outputs:
- result: float32 [2048, 5120], P(('section', 'hid'), 'mod')
The draws below stay inside these ranges and needn't reach their ends.
All inputs are finite; a program needn't handle non-finite values.
Results may differ from the reference program's by a relative error of at most 0.006.
Values may be sent and summed in bfloat16 or wider, within the bound.
A program may use at most 128 MiB of HBM per device.

```python
import jax
import jax.numpy as jnp
from jax import lax

D = 5120
FF = 13824
ROWS = 2048
N_SECTION = 2
N_HID = 8
N_MOD = 2


def draw_tokens(key, part):
    keys = jax.random.split(jax.random.fold_in(key, 7), 4)
    columns = jnp.arange(D, dtype=jnp.float32) / D
    col_scale = jnp.exp(jnp.log(3.0) * columns) * jnp.exp(jax.random.uniform(keys[0], (D,), jnp.float32, 0.0, jnp.log(3.3)))
    base = jnp.clip(jax.random.normal(keys[1], (ROWS, D), jnp.float32), -5.0, 5.0)
    row_scale = jnp.exp(jax.random.uniform(keys[3], (ROWS, 1), jnp.float32, jnp.log(0.3), jnp.log(3.0)))
    return base * row_scale * col_scale


def levels(own_key, dims, cuts, least, high):
    def one(dim, parts):
        steps = jax.random.uniform(jax.random.fold_in(jax.random.fold_in(own_key, 6), dim), (parts,), jnp.float32, least / len(cuts), high / len(cuts))
        return jnp.repeat(jnp.exp(steps), dims[dim] // parts).reshape((-1,) + (1,) * (len(dims) - dim - 1))

    level = one(*cuts[0])
    for cut in cuts[1:]:
        level = level * one(*cut)
    return level


def gaussian(rng, dims, scale, limit, cuts=(), held_as=jnp.bfloat16):
    level = levels(rng, dims, cuts, -0.22, 0.18) if cuts else 1.0
    entries = jax.random.normal(rng, dims, jnp.float32) * scale * level
    return jnp.minimum(jnp.maximum(entries, -limit), limit).astype(held_as)


def setup_inputs(seed: int = 0) -> dict:
    splits = jax.random.split(jax.random.key(seed), 10)
    return {
        "tokens": draw_tokens(jax.random.fold_in(splits[9], 71), 0),
        "gain_first": jnp.clip(1.0 + 0.18 * jax.random.normal(splits[1], (D,), jnp.float32), 0.1, 1.9),
        "gate_first": gaussian(splits[2], (D, FF), D ** -0.5, 0.078125, ((0, 2), (1, 8))),
        "up_first": gaussian(splits[3], (D, FF), D ** -0.5, 0.078125, ((0, 2), (1, 8))),
        "down_first": gaussian(splits[4], (FF, D), FF ** -0.5, 0.0546875, ((0, 8), (1, 2))),
        "gain_second": jnp.clip(1.0 + 0.18 * jax.random.normal(splits[5], (D,), jnp.float32), 0.1, 1.9),
        "gate_second": gaussian(splits[6], (D, FF), D ** -0.5, 0.078125, ((0, 2), (1, 16))),
        "up_second": gaussian(splits[7], (D, FF), D ** -0.5, 0.078125, ((0, 2), (1, 16))),
        "down_second": gaussian(splits[8], (FF, D), FF ** -0.5, 0.0546875, ((0, 16), (1, 2))),
    }


epsilon = 1e-06

def rounded_partial(normed, weight, first, block_width):
    product = jnp.dot(normed[:, first:first + block_width], weight[first:first + block_width, :], preferred_element_type=jnp.float32)
    return lax.optimization_barrier(product.astype(jnp.bfloat16)).astype(jnp.float32)

def apply_block(stream, gain, w_gate, w_up, w_down, down_groups):
    mean_sq = lax.optimization_barrier(jnp.mean(stream * stream, axis=1, keepdims=True))
    normed = (stream * lax.rsqrt(mean_sq + epsilon) * gain).astype(jnp.bfloat16)
    block_width = D // N_MOD
    gate_sum = jnp.zeros((stream.shape[0], w_gate.shape[1]), jnp.float32)
    up_sum = jnp.zeros((stream.shape[0], w_up.shape[1]), jnp.float32)
    for group in range(N_MOD):
        first = group * block_width
        gate_sum = gate_sum + rounded_partial(normed, w_gate, first, block_width)
        up_sum = up_sum + rounded_partial(normed, w_up, first, block_width)
    activated = (jax.nn.silu(gate_sum) * up_sum).astype(jnp.bfloat16)
    unit_width = FF // down_groups
    output = stream
    for group in range(down_groups):
        output = output + rounded_partial(activated, w_down, group * unit_width, unit_width)
    return output

def reference(tokens, gain_first, gate_first, up_first, down_first, gain_second, gate_second, up_second, down_second):
    middle = apply_block(tokens, gain_first, gate_first, up_first, down_first, N_HID)
    return apply_block(middle, gain_second, gate_second, up_second, down_second, N_SECTION * N_HID)
```

```python
import jax
import jax.numpy as jnp
from jax import lax
from jax.sharding import PartitionSpec as P

epsilon = 1e-06


def axis_size(mesh, name):
    return mesh.shape[name]


def shift(value, axis, size, distance):
    return lax.ppermute(value, axis, [(j, (j + distance) % size) for j in range(size)])


def snake(size):
    return list(range(0, size, 2)) + list(reversed(range(1, size, 2)))


def ring_step(value, size, direction):
    order = snake(size)
    return lax.ppermute(
        value, "hid", [(order[i], order[(i + direction) % size]) for i in range(size)]
    )


def mod_total(value, n_mod):
    if n_mod > 2:
        return lax.psum(value, "mod")
    return value + sum(shift(value, "mod", n_mod, d) for d in range(1, n_mod))


def scale_rows(stream, gain, n_mod):
    square_sum = mod_total(jnp.sum(stream * stream, axis=1), n_mod)
    mean = square_sum[:, None] / (stream.shape[1] * n_mod)
    return (stream * lax.rsqrt(mean + epsilon) * gain).astype(jnp.bfloat16)


def product(rows, weight):
    return jnp.dot(rows, weight, preferred_element_type=jnp.float32)


def swiglu(gate, up):
    return (jax.nn.silu(gate) * up).astype(jnp.bfloat16)


def chunk_terms(rows, w_gate, w_up, w_down):
    half = rows.shape[0] // 2

    def summed(weight):
        partial = product(rows, weight).astype(jnp.bfloat16)
        arrived = shift(partial[:half], "mod", 2, 1)
        return partial[half:].astype(jnp.float32) + arrived.astype(jnp.float32)

    activated = swiglu(summed(w_gate), summed(w_up))
    other = shift(activated, "mod", 2, 1)
    return product(jnp.concatenate([other, activated], axis=0), w_down)


def trade(first, second, swap):
    return jnp.where(swap, second, first), jnp.where(swap, first, second)


def section_rows(rows, n_section):
    return jnp.concatenate(
        [rows] + [shift(rows, "section", n_section, d) for d in range(1, n_section)], axis=0
    )


def section_sum(terms, n_section):
    own = terms.shape[0] // n_section
    total = terms[:own]
    for d in range(1, n_section):
        back = terms[d * own : (d + 1) * own].astype(jnp.bfloat16)
        total = total + shift(back, "section", n_section, -d).astype(jnp.float32)
    return total


def gathered_block(stream, gain, w_gate, w_up, w_down, n_section, n_hid, n_mod):
    axes = ("section", "hid") if n_section > 1 else "hid"
    rows = lax.all_gather(scale_rows(stream, gain, n_mod), axes, axis=0, tiled=True)
    partial = jnp.concatenate(
        [product(rows, w).astype(jnp.bfloat16) for w in (w_gate, w_up)], axis=1
    )
    summed = lax.psum_scatter(partial, "mod", scatter_dimension=0, tiled=True)
    gate, up = jnp.split(summed.astype(jnp.float32), 2, axis=1)
    activated = lax.all_gather(swiglu(gate, up), "mod", axis=0, tiled=True)
    terms = product(activated, w_down).astype(jnp.bfloat16)
    return stream + lax.psum_scatter(
        terms, axes, scatter_dimension=0, tiled=True
    ).astype(jnp.float32)


def ring_block(stream, gain, w_gate, w_up, w_down, n_section, n_hid, n_mod):
    own = scale_rows(stream, gain, n_mod)
    rows = own.shape[0]
    half = rows // 2
    pairs = (n_hid - 1) // 2
    chunks = {0: own}
    forward = backward = own
    for k in range(1, pairs + 1):
        forward = ring_step(forward, n_hid, 1)
        backward = ring_step(backward, n_hid, -1)
        chunks[k] = jnp.concatenate([forward, backward], axis=0)
    far = n_hid // 2
    if n_hid % 2 == 0:
        chunks[far] = jnp.concatenate(
            [
                ring_step(forward[:half], n_hid, 1),
                ring_step(backward[half:], n_hid, -1),
            ],
            axis=0,
        )

    near = min(1, pairs)
    order = list(range(near + 1)) + list(range(far, near, -1))
    swap = lax.axis_index("mod") == 0
    terms = {}
    for k in order:
        middle = chunks[k].shape[0] // 2
        sent, kept = trade(chunks[k][:middle], chunks[k][middle:], swap)
        sent, kept = section_rows(sent, n_section), section_rows(kept, n_section)
        part = chunk_terms(jnp.concatenate([sent, kept], axis=0), w_gate, w_up, w_down)
        middle = part.shape[0] // 2
        sent = section_sum(part[:middle], n_section)
        kept = section_sum(part[middle:], n_section)
        terms[k] = jnp.concatenate(trade(sent, kept, swap), axis=0)

    forward = backward = None
    if n_hid % 2 == 0:
        forward = ring_step(terms[far][half:].astype(jnp.bfloat16), n_hid, 1)
        backward = ring_step(terms[far][:half].astype(jnp.bfloat16), n_hid, -1)
    for k in range(pairs, 0, -1):
        to_back, to_front = terms[k][:rows], terms[k][rows:]
        if forward is not None:
            if forward.shape[0] < rows:
                to_front = jnp.concatenate(
                    [to_front[:half], to_front[half:] + forward.astype(jnp.float32)], axis=0
                )
                to_back = jnp.concatenate(
                    [to_back[:half] + backward.astype(jnp.float32), to_back[half:]], axis=0
                )
            else:
                to_front = to_front + forward.astype(jnp.float32)
                to_back = to_back + backward.astype(jnp.float32)
        forward = ring_step(to_front.astype(jnp.bfloat16), n_hid, 1)
        backward = ring_step(to_back.astype(jnp.bfloat16), n_hid, -1)
    total = stream + terms[0]
    if forward is None:
        return total
    if forward.shape[0] < rows:
        return total + jnp.concatenate([backward, forward], axis=0).astype(jnp.float32)
    return total + forward.astype(jnp.float32) + backward.astype(jnp.float32)


def solution(mesh):
    n_section, n_hid, n_mod = (axis_size(mesh, a) for a in ("section", "hid", "mod"))

    block = ring_block if n_mod == 2 and n_hid <= 8 else gathered_block

    def per_device(
        tokens,
        gain_first,
        gate_first,
        up_first,
        down_first,
        gain_second,
        gate_second,
        up_second,
        down_second,
    ):
        middle = block(tokens, gain_first, gate_first, up_first, down_first, 1, n_hid, n_mod)
        return block(
            middle, gain_second, gate_second, up_second, down_second, n_section, n_hid, n_mod
        )

    in_specs = (
        P(("section", "hid"), "mod"),
        P("mod"),
        P("mod", "hid"),
        P("mod", "hid"),
        P("hid", "mod"),
        P("mod"),
        P("mod", ("section", "hid")),
        P("mod", ("section", "hid")),
        P(("section", "hid"), "mod"),
    )
    out_specs = P(("section", "hid"), "mod")
    return jax.shard_map(
        per_device, mesh=mesh, in_specs=in_specs, out_specs=out_specs, check_vma=False
    )
```

```python
import jax
import jax.numpy as jnp
from jax import lax
from jax.sharding import PartitionSpec as P


epsilon = 1e-06


def axis_size(mesh, name):
    return mesh.shape[name]


def shift(value, axis, size, distance):
    return lax.ppermute(value, axis, [(j, (j + distance) % size) for j in range(size)])


def snake(size):
    return list(range(0, size, 2)) + list(reversed(range(1, size, 2)))


def ring_step(value, size, direction):
    order = snake(size)
    return lax.ppermute(
        value, "hid", [(order[i], order[(i + direction) % size]) for i in range(size)]
    )


def mod_total(value, n_mod):
    if n_mod > 2:
        return lax.psum(value, "mod")
    return value + sum(shift(value, "mod", n_mod, d) for d in range(1, n_mod))


def scale_rows(stream, gain, n_mod):
    square_sum = mod_total(jnp.sum(stream * stream, axis=1), n_mod)
    mean = square_sum[:, None] / (stream.shape[1] * n_mod)
    return (stream * lax.rsqrt(mean + epsilon) * gain).astype(jnp.bfloat16)


def product(rows, weight):
    return jnp.dot(rows, weight, preferred_element_type=jnp.float32)


def swiglu(gate, up):
    return (jax.nn.silu(gate) * up).astype(jnp.bfloat16)


def chunk_terms(rows, w_gate, w_up, w_down):
    half = rows.shape[0] // 2

    def summed(weight):
        partial = product(rows, weight).astype(jnp.bfloat16)
        arrived = shift(partial[:half], "mod", 2, 1)
        return partial[half:].astype(jnp.float32) + arrived.astype(jnp.float32)

    activated = swiglu(summed(w_gate), summed(w_up))
    other = shift(activated, "mod", 2, 1)
    return product(jnp.concatenate([other, activated], axis=0), w_down)


def trade(first, second, swap):
    return jnp.where(swap, second, first), jnp.where(swap, first, second)


def section_chunks(rows, n_section):
    return [rows] + [shift(rows, "section", n_section, -d) for d in range(1, n_section)]


def section_sum(terms, n_section):
    total = terms[0]
    for d in range(1, n_section):
        back = terms[d].astype(jnp.bfloat16)
        total = total + shift(back, "section", n_section, d).astype(jnp.float32)
    return total


def gathered_block(stream, gain, w_gate, w_up, w_down, n_section, n_hid, n_mod):
    axes = ("section", "hid") if n_section > 1 else "hid"
    rows = lax.all_gather(scale_rows(stream, gain, n_mod), axes, axis=0, tiled=True)
    partial = jnp.concatenate(
        [product(rows, w).astype(jnp.bfloat16) for w in (w_gate, w_up)], axis=1
    )
    summed = lax.psum_scatter(partial, "mod", scatter_dimension=0, tiled=True)
    gate, up = jnp.split(summed.astype(jnp.float32), 2, axis=1)
    activated = lax.all_gather(swiglu(gate, up), "mod", axis=0, tiled=True)
    terms = product(activated, w_down).astype(jnp.bfloat16)
    return stream + lax.psum_scatter(
        terms, axes, scatter_dimension=0, tiled=True
    ).astype(jnp.float32)


def chunk_order(n_hid):
    order = list(range((n_hid - 1) // 2 + 1))
    if n_hid % 2 == 0:
        order.insert(max(1, len(order) - 1), n_hid // 2)
    return order


def ring_block(stream, gain, w_gate, w_up, w_down, n_section, n_hid, n_mod):
    own = scale_rows(stream, gain, n_mod)
    rows = own.shape[0]
    half = rows // 2
    pairs = (n_hid - 1) // 2
    chunks = {0: own}
    forward = backward = own
    for k in range(1, pairs + 1):
        forward = ring_step(forward, n_hid, 1)
        backward = ring_step(backward, n_hid, -1)
        chunks[k] = jnp.concatenate([forward, backward], axis=0)
    far = n_hid // 2
    if n_hid % 2 == 0:
        last = [ring_step(forward[:half], n_hid, 1), ring_step(backward[half:], n_hid, -1)]
        chunks[far] = jnp.concatenate(last, axis=0)

    order = chunk_order(n_hid)
    swap = lax.axis_index("mod") == 0
    terms = {}
    for k in order:
        middle = chunks[k].shape[0] // 2
        traded = [
            trade(chunk[:middle], chunk[middle:], swap)
            for chunk in section_chunks(chunks[k], n_section)
        ]
        rows_in = jnp.concatenate([sent for sent, _ in traded] + [kept for _, kept in traded], axis=0)
        part = chunk_terms(rows_in, w_gate, w_up, w_down)
        part = part.reshape(2, n_section, middle, part.shape[1])
        terms[k] = section_sum(
            [
                jnp.concatenate(trade(part[0, d], part[1, d], swap), axis=0)
                for d in range(n_section)
            ],
            n_section,
        )

    forward = backward = None
    if n_hid % 2 == 0:
        forward = ring_step(terms[far][half:].astype(jnp.bfloat16), n_hid, 1)
        backward = ring_step(terms[far][:half].astype(jnp.bfloat16), n_hid, -1)
    for k in range(pairs, 0, -1):
        to_back, to_front = terms[k][:rows], terms[k][rows:]
        if forward is not None:
            if forward.shape[0] < rows:
                to_front = jnp.concatenate(
                    [to_front[:half], to_front[half:] + forward.astype(jnp.float32)], axis=0
                )
                to_back = jnp.concatenate(
                    [to_back[:half] + backward.astype(jnp.float32), to_back[half:]], axis=0
                )
            else:
                to_front = to_front + forward.astype(jnp.float32)
                to_back = to_back + backward.astype(jnp.float32)
        forward = ring_step(to_front.astype(jnp.bfloat16), n_hid, 1)
        backward = ring_step(to_back.astype(jnp.bfloat16), n_hid, -1)
    total = stream + terms[0]
    if forward is None:
        return total
    if forward.shape[0] < rows:
        return total + jnp.concatenate([backward, forward], axis=0).astype(jnp.float32)
    return total + forward.astype(jnp.float32) + backward.astype(jnp.float32)


def solution(mesh):
    n_section, n_hid, n_mod = (axis_size(mesh, a) for a in ("section", "hid", "mod"))

    block = ring_block if n_mod == 2 and n_hid <= 8 else gathered_block

    def per_device(
        tokens,
        gain_first,
        gate_first,
        up_first,
        down_first,
        gain_second,
        gate_second,
        up_second,
        down_second,
    ):
        middle = block(tokens, gain_first, gate_first, up_first, down_first, 1, n_hid, n_mod)
        return block(
            middle, gain_second, gate_second, up_second, down_second, n_section, n_hid, n_mod
        )

    in_specs = (
        P(("section", "hid"), "mod"),
        P("mod"),
        P("mod", "hid"),
        P("mod", "hid"),
        P("hid", "mod"),
        P("mod"),
        P("mod", ("section", "hid")),
        P("mod", ("section", "hid")),
        P(("section", "hid"), "mod"),
    )
    out_specs = P(("section", "hid"), "mod")
    program = jax.shard_map(
        per_device, mesh=mesh, in_specs=in_specs, out_specs=out_specs, check_vma=False
    )
    if block is gathered_block:
        return program
    return program
```
